32 devices in a mesh: aa: 8 (over y, x, core), col: 4 (over z).
Axes of the slice: x: 2, y: 2, z: 4, core: 2. Of those that a mesh axis runs over, the one named last changes fastest.
Arguments:
- fit_ac: float32 [512, 512, 2048], P('aa', 'col'), may hold values from -0.125 to 0.125
- fit_bd: float32 [2048, 1024], P(('aa', 'col')), may hold values from -6 to 6
- amplitudes: float32 [2, 32, 512, 256], P(None, 'aa', 'col'), may hold values from -0.046875 to 0.046875
Outputs:
- residual: float32 [2, 16, 512, 256], P(None, 'col', 'aa')
The draws below stay inside these ranges and needn't reach their ends.
All inputs are finite; a program needn't handle non-finite values.
Results may differ from the reference program's by a relative error of at most 0.0003.
Values sent between devices are 32-bit elements; how exact they have to be, the bound alone decides.
A program may use at most 192 MiB of HBM per device.

```python
import jax
import jax.numpy as jnp
from jax import lax

V = 512
NQ = 2048
KB = 2
NB = 16
ND = 32
P_SIZE = 256
N_AA = 8


def levels(own_key, extent, cuts, low, top_value):
    gain = 1.0
    for axis_at, parts in cuts:
        steps = jax.random.uniform(jax.random.fold_in(jax.random.fold_in(own_key, 6), axis_at), (parts,), jnp.float32, low / len(cuts), top_value / len(cuts))
        gain = gain * jnp.repeat(jnp.exp(steps), extent[axis_at] // parts).reshape((-1,) + (1,) * (len(extent) - 1 - axis_at))
    return gain


def normal_values(stream_key, extent, spread, most, cuts=(), held_as=jnp.bfloat16):
    factor_of = levels(stream_key, extent, cuts, -0.22, 0.18) if cuts else 1.0
    entries = jax.random.normal(stream_key, extent, jnp.float32) * spread * factor_of
    return jnp.minimum(jnp.maximum(entries, -most), most).astype(held_as)


def setup_inputs(seed: int = 0) -> dict:
    splits = jax.random.split(jax.random.key(seed), 4)
    return {
        "fit_ac": normal_values(splits[0], (V, V, NQ), NQ ** -0.5, 0.125, ((0, 8), (1, 4)), jnp.float32),
        "fit_bd": normal_values(splits[1], (NQ, KB * NB * ND), 1.0, 6.0, ((0, 32),), jnp.float32),
        "amplitudes": normal_values(splits[2], (KB, ND, V, P_SIZE), (V * ND) ** -0.5, 0.046875, ((1, 8), (2, 4)), jnp.float32),
    }


def reference(fit_ac, fit_bd, amplitudes):
    a_block = V // N_AA

    def one_block(index):
        start = (index * a_block).astype(jnp.int32)
        piece = lax.dynamic_slice_in_dim(fit_ac, start, a_block, 0)
        integrals = jnp.dot(piece.reshape(a_block * V, NQ), fit_bd, precision=lax.Precision.HIGHEST, preferred_element_type=jnp.float32)
        integrals = integrals.reshape(a_block, V, KB, NB, ND)
        return jnp.einsum("kdcp,ackbd->kbap", amplitudes, integrals, precision=lax.Precision.HIGHEST)

    pieces = lax.map(one_block, jnp.arange(V // a_block, dtype=jnp.int32))
    return pieces.transpose(1, 2, 0, 3, 4).reshape(KB, NB, V, P_SIZE)
```

```python
import functools

import jax
import jax.numpy as jnp
from jax import lax
from jax.experimental import pallas as pl
from jax.experimental.pallas import tpu as pltpu
from jax.sharding import PartitionSpec as P


F32 = jnp.float32
BF16 = jnp.bfloat16
F8 = jnp.float8_e4m3fn
NT = (((1,), (1,)), ((), ()))
VMEM_LIMIT = 60 * 2**20

A_HI, A_LO, B_HI, B_LO = 2.0**11, 2.0**20, 2.0**5, 2.0**14
UNDO = 2.0**-25


def split(value):
    high = value.astype(BF16)
    return high, value - high.astype(F32)


def exchange(block, axis, size, strides):
    blocks, offsets = [block], [0]
    for stride in strides:
        pairs = [(i, i ^ stride) for i in range(size)]
        blocks += [lax.ppermute(one, axis, pairs) for one in blocks]
        offsets += [one ^ stride for one in offsets]
    return blocks, offsets


def prepare_kernel(offsets, parts, index_ref, *refs):
    ins, (high_ref, low8_ref, high8_ref) = refs[:-3], refs[-3:]
    count = len(offsets[0])
    for part in range(parts):
        for at in range(count):
            block = ins[part * count + at]
            depth, rows = block.shape
            value = block[...].T
            high, low = split(value)
            start = pl.multiple_of((index_ref[0] ^ offsets[part][at]) * depth, depth)
            to = (pl.ds(part * rows, rows), pl.ds(start, depth))
            high_ref[to] = high
            low8_ref[to] = (low * B_LO).astype(F8)
            high8_ref[to] = (value * B_HI).astype(F8)


def integrals_kernel(a_ref, high_ref, low8_ref, high8_ref, out_ref):
    rows = a_ref.shape[0] * a_ref.shape[1]
    value = a_ref[...].reshape(rows, a_ref.shape[2])
    high, low = split(value)
    dot = functools.partial(lax.dot_general, dimension_numbers=NT, preferred_element_type=F32)
    small = dot(low8_ref[...], (value * A_HI).astype(F8))
    small += dot(high8_ref[...], (low * A_LO).astype(F8))
    out_ref[...] = dot(high_ref[...], high) + small * UNDO


def ladder_kernel(offsets, index_ref, x_ref, *refs):
    ins, out_ref, wide = refs[:-2], refs[-2], refs[-1]
    d_local, c_local, pairs = ins[0].shape
    b_size = x_ref.shape[1]
    rows = wide.shape[0] // b_size
    for at, offset in enumerate(offsets):
        for d in range(d_local):
            piece = x_ref[(index_ref[0] ^ offset) * d_local + d]
            col = (at * d_local + d) * c_local
            for a in range(rows):
                wide[a * b_size : (a + 1) * b_size, col : col + c_local] = piece[:, a * c_local : (a + 1) * c_local]
    dot = functools.partial(jnp.dot, preferred_element_type=F32)
    total = None
    span = d_local * c_local
    for at in range(len(offsets)):
        x_high, x_low = split(wide[:, at * span : (at + 1) * span])
        t_high, t_low = split(ins[at][...].reshape(span, pairs))
        x_low, t_low = x_low.astype(BF16), t_low.astype(BF16)
        term = dot(x_high, t_high) + (dot(x_low, t_high) + dot(x_high, t_low))
        total = term if total is None else total + term
    out_ref[...] = total


def shards(n_aa, n_col, fit_ac, fit_bd, amplitudes):
    a_local, c_local, count_q = fit_ac.shape
    blocks, d_local, _, pairs = amplitudes.shape
    d_size = d_local * n_aa
    columns = fit_bd.shape[1]
    b_size = columns // (blocks * d_size)
    aa = lax.axis_index("aa").astype(jnp.int32)
    col = lax.axis_index("col")
    index = aa[None]
    own = fit_bd.reshape(-1, blocks, b_size, d_size).transpose(1, 0, 3, 2)
    own = own.reshape(blocks, -1, d_size * b_size)
    far = [1 << bit for bit in range(1, n_aa.bit_length() - 1)]
    orders = [far + [1], far[::-1] + [1]]

    parts = [own]
    for step in range(1, n_col):
        parts.append(lax.ppermute(own, "col", [(i, (i + step) % n_col) for i in range(n_col)]))
    grouped = jnp.zeros((n_col,) + own.shape, F32)
    for step, part in enumerate(parts):
        grouped = lax.dynamic_update_index_in_dim(grouped, part, (col - step) % n_col, 0)
    grouped = grouped.transpose(1, 0, 2, 3).reshape(blocks, -1, d_size * b_size)
    bd, bd_at, t, t_at = [], [], [], []
    for k in range(blocks):
        got, at = exchange(grouped[k], "aa", n_aa, orders[k % 2])
        bd += got
        bd_at.append(at)
    held = lax.optimization_barrier((amplitudes, grouped))[0]
    for k in range(blocks):
        got, at = exchange(held[k], "aa", n_aa, orders[k % 2])
        t.append(got)
        t_at.append(at)

    smem = pl.BlockSpec(memory_space=pltpu.SMEM)
    vmem = pl.BlockSpec(memory_space=pltpu.VMEM)
    limit = pltpu.CompilerParams(vmem_limit_bytes=VMEM_LIMIT)
    like = functools.partial(jax.ShapeDtypeStruct, (columns, count_q))
    factors = pl.pallas_call(
        functools.partial(prepare_kernel, bd_at, blocks),
        in_specs=[smem] + [vmem] * len(bd),
        out_specs=[vmem] * 3,
        out_shape=[like(BF16), like(F8), like(F8)],
        compiler_params=limit,
    )(index, *bd)

    rows = max(1, min(a_local, 512 // c_local))
    whole = pl.BlockSpec((columns, count_q), lambda i: (0, 0), pipeline_mode=pl.Buffered(1))
    work = columns * a_local * c_local
    integrals = pl.pallas_call(
        integrals_kernel,
        grid=(a_local // rows,),
        in_specs=[pl.BlockSpec((rows, c_local, count_q), lambda i: (i, 0, 0))] + [whole] * 3,
        out_specs=pl.BlockSpec((columns, rows * c_local), lambda i: (0, i)),
        out_shape=jax.ShapeDtypeStruct((columns, a_local * c_local), F32),
        compiler_params=limit,
        cost_estimate=pl.CostEstimate(
            flops=4 * work * count_q, bytes_accessed=4 * (fit_ac.size + work), transcendentals=0
        ),
    )(fit_ac, *factors)
    integrals = integrals.reshape(blocks * d_size, b_size, a_local * c_local)

    rows = min(a_local, 16)
    outs = []
    for k in range(blocks):
        partial_value = pl.pallas_call(
            functools.partial(ladder_kernel, t_at[k]),
            grid=(a_local // rows,),
            in_specs=[smem, pl.BlockSpec((d_size, b_size, rows * c_local), lambda i, k=k: (k, 0, i))]
            + [pl.BlockSpec(t[k][0].shape, lambda i: (0, 0, 0), pipeline_mode=pl.Buffered(1))] * n_aa,
            out_specs=pl.BlockSpec((rows * b_size, pairs), lambda i: (i, 0)),
            out_shape=jax.ShapeDtypeStruct((a_local * b_size, pairs), F32),
            scratch_shapes=[pltpu.VMEM((rows * b_size, d_size * c_local), F32)],
            compiler_params=limit,
            cost_estimate=pl.CostEstimate(
                flops=6 * work // blocks * pairs, bytes_accessed=4 * work // blocks, transcendentals=0
            ),
        )(index, integrals, *t[k])
        value = partial_value.reshape(a_local, n_col, b_size // n_col, pairs).transpose(1, 2, 0, 3)
        total = lax.dynamic_index_in_dim(value, col, 0, keepdims=False)
        for step in range(1, n_col):
            piece = lax.dynamic_index_in_dim(value, (col + step) % n_col, 0, keepdims=False)
            total = total + lax.ppermute(piece, "col", [(i, (i + step) % n_col) for i in range(n_col)])
        outs.append(total)
    return jnp.stack(outs)


def solution(mesh):
    placed = (P("aa", "col", None), P(("aa", "col"), None), P(None, "aa", "col", None))
    body = functools.partial(shards, mesh.shape["aa"], mesh.shape["col"])
    return jax.shard_map(
        body, mesh=mesh, in_specs=placed, out_specs=P(None, "col", "aa", None), check_vma=False
    )
```
